32 devices in a mesh: space: 8 (over z, x), field: 4 (over y, core).
Axes of the slice: x: 2, y: 2, z: 4, core: 2. Of those that a mesh axis runs over, the one named last changes fastest.
Arguments:
- composition_vector: float32 [4, 32, 32, 16, 128], P('field', None, 'space'), may hold values from -6 to 6
- filtered_motion: float32 [3, 32, 16, 128], P(None, 'space', 'field'), may hold values from -1.8 to 1.8
- spreading_strength: float32 [32, 16, 128], P('space', 'field'), may hold values from 0.02 to 0.12
- blend_relax_multiplier: float32 [32, 16, 128], P('space', 'field'), may hold values from 0.2 to 0.9
- thermal_level: float32 [32, 16, 128], P('space', 'field'), may hold values from 0.5 to 2
- brownian_jumps: float32 [2, 4, 3], P(None, 'field'), may hold values from -2.5 to 2.5
- left_bilinear_weights: bfloat16 [206, 32], replicated, may hold values from -1 to 1
- right_bilinear_weights: bfloat16 [206, 32], replicated, may hold values from -1 to 1
- species_yield_weights: bfloat16 [32, 206], replicated, may hold values from -0.4375 to 0.4375
- arrhenius_prefactor: float32 [206], replicated, may hold values from 0.3 to 3
- ignition_energy_ratio: float32 [206], replicated, may hold values from 0.2 to 2
Outputs:
- result: float32 [4, 32, 32, 16, 128], P('field', None, 'space')
The draws below stay inside these ranges and needn't reach their ends.
All inputs are finite; a program needn't handle non-finite values.
Results may differ from the reference program's by a relative error of at most 0.00068.
Values sent between devices are 32-bit elements; how exact they have to be, the bound alone decides.
A program may use at most 64 MiB of HBM per device.

```python
import math
import jax
import jax.numpy as jnp
from jax import lax

S = 32
R = 206
GRID_COUNT_Y = 16
GRID_COUNT_Z = 128
STEPS = 2
SUB = 5
FIELDS = 4
GRID_COUNT_X = 32


def shard_levels(own_key, extent, shards, smallest, high):
    factor_of = 1.0
    for position, blocks in shards:
        heights = jax.random.uniform(jax.random.fold_in(jax.random.fold_in(own_key, 6), position), (blocks,), jnp.float32, smallest / len(shards), high / len(shards))
        factor_of = factor_of * jnp.repeat(jnp.exp(heights), extent[position] // blocks).reshape((-1,) + (1,) * (len(extent) - 1 - position))
    return factor_of


def bell_draw(key, shape, spread, reach, cuts=(), dtype=jnp.bfloat16):
    array = spread * jax.random.normal(key, shape, jnp.float32)
    if cuts:
        array = array * shard_levels(key, shape, cuts, -0.22, 0.18)
    return jnp.clip(array, -reach, reach).astype(dtype)


def setup_inputs(seed: int = 0) -> dict:
    key_of = jax.random.split(jax.random.key(seed), 12)
    composition_vector = bell_draw(key_of[0], (FIELDS, S, GRID_COUNT_X, GRID_COUNT_Y, GRID_COUNT_Z), 1.0, 6.0, ((0, 4), (2, 8)), jnp.float32)
    filtered_motion = bell_draw(key_of[1], (3, GRID_COUNT_X, GRID_COUNT_Y, GRID_COUNT_Z), 0.3, 1.8, ((1, 8), (2, 4)), jnp.float32)
    spreading_strength = jnp.clip(0.02 + 0.09999999776482582 * jax.random.uniform(key_of[2], (GRID_COUNT_X, GRID_COUNT_Y, GRID_COUNT_Z), jnp.float32) ** shard_levels(key_of[2], (GRID_COUNT_X, GRID_COUNT_Y, GRID_COUNT_Z), ((0, 8), (1, 4)), -0.2, 0.2), 0.02, 0.12)
    blend_relax_multiplier = jnp.clip(0.2 + 0.7 * jax.random.uniform(key_of[3], (GRID_COUNT_X, GRID_COUNT_Y, GRID_COUNT_Z), jnp.float32) ** shard_levels(key_of[3], (GRID_COUNT_X, GRID_COUNT_Y, GRID_COUNT_Z), ((0, 8), (1, 4)), -0.2, 0.2), 0.2, 0.9)
    thermal_level = jnp.clip(0.5 + 1.5 * jax.random.uniform(key_of[4], (GRID_COUNT_X, GRID_COUNT_Y, GRID_COUNT_Z), jnp.float32) ** shard_levels(key_of[4], (GRID_COUNT_X, GRID_COUNT_Y, GRID_COUNT_Z), ((0, 8), (1, 4)), -0.2, 0.2), 0.5, 2.0)
    brownian_jumps = bell_draw(key_of[5], (STEPS, FIELDS, 3), 0.4, 2.5, ((1, 4),), jnp.float32)
    left_bilinear_weights = bell_draw(key_of[6], (R, S), S ** -0.5, 1.0)
    right_bilinear_weights = bell_draw(key_of[7], (R, S), S ** -0.5, 1.0)
    species_yield_weights = bell_draw(key_of[8], (S, R), R ** -0.5, 0.4375)
    arrhenius_prefactor = jnp.clip(jnp.exp(jax.random.uniform(key_of[9], (R,), jnp.float32, math.log(0.3), math.log(3.0))), 0.3, 3.0)
    ignition_energy_ratio = jnp.clip(jnp.exp(jax.random.uniform(key_of[10], (R,), jnp.float32, math.log(0.2), math.log(2.0))), 0.2, 2.0)
    return dict(composition_vector=composition_vector, filtered_motion=filtered_motion, spreading_strength=spreading_strength, blend_relax_multiplier=blend_relax_multiplier, thermal_level=thermal_level, brownian_jumps=brownian_jumps, left_bilinear_weights=left_bilinear_weights, right_bilinear_weights=right_bilinear_weights, species_yield_weights=species_yield_weights, arrhenius_prefactor=arrhenius_prefactor, ignition_energy_ratio=ignition_energy_ratio)


chem_step = 0.2

def transport(padded, current, mean, filtered_motion, spreading_strength, mixing, wiener):
    x_plus = padded[:, 2:]
    x_minus = padded[:, :-2]
    y_plus = jnp.roll(current, -1, 2)
    y_minus = jnp.roll(current, 1, 2)
    z_plus = jnp.roll(current, -1, 3)
    z_minus = jnp.roll(current, 1, 3)
    grad_x = 0.5 * (x_plus - x_minus)
    grad_y = 0.5 * (y_plus - y_minus)
    grad_z = 0.5 * (z_plus - z_minus)
    laplace = x_plus + x_minus + y_plus + y_minus + z_plus + z_minus - 6.0 * current
    advect = filtered_motion[0] * grad_x + filtered_motion[1] * grad_y + filtered_motion[2] * grad_z
    noise = jnp.sqrt(2.0 * spreading_strength) * (wiener[0] * grad_x + wiener[1] * grad_y + wiener[2] * grad_z)
    return current - advect + spreading_strength * laplace + noise - mixing * (current - mean)

def react(block, arrhenius, left_bilinear_weights, right_bilinear_weights, species_yield_weights):
    for substep in range(SUB):
        lowered = block.astype(jnp.bfloat16)
        forward = jnp.dot(left_bilinear_weights, lowered, preferred_element_type=jnp.float32)
        backward = jnp.dot(right_bilinear_weights, lowered, preferred_element_type=jnp.float32)
        saturation = 1.0 + forward * forward + backward * backward
        rates = (arrhenius * forward * backward / saturation).astype(jnp.bfloat16)
        block = block + chem_step * jnp.dot(species_yield_weights, rates, preferred_element_type=jnp.float32)
    return block

def kinetic_yield_term(carried_ensemble, thermal_level, arrhenius_prefactor, ignition_energy_ratio, left_bilinear_weights, right_bilinear_weights, species_yield_weights):
    species_count, planes, vertical_extent, streamwise_extent = carried_ensemble.shape

    def one_plane(plane_index, current):
        starting_ensemble = jnp.asarray(plane_index).astype(jnp.int32)
        block = lax.dynamic_slice_in_dim(current, starting_ensemble, 1, 1).reshape(species_count, vertical_extent * streamwise_extent)
        enthalpy_output = lax.dynamic_slice_in_dim(thermal_level, starting_ensemble, 1, 0).reshape(1, vertical_extent * streamwise_extent)
        arrhenius = arrhenius_prefactor[:, None] * jnp.exp(-ignition_energy_ratio[:, None] / enthalpy_output)
        reacted = react(block, arrhenius, left_bilinear_weights, right_bilinear_weights, species_yield_weights)
        reacted = reacted.reshape(species_count, 1, vertical_extent, streamwise_extent)
        return lax.dynamic_update_slice_in_dim(current, reacted, starting_ensemble, 1)
    return lax.fori_loop(0, planes, one_plane, carried_ensemble)

def reference(composition_vector, filtered_motion, spreading_strength, blend_relax_multiplier, thermal_level, brownian_jumps, left_bilinear_weights, right_bilinear_weights, species_yield_weights, arrhenius_prefactor, ignition_energy_ratio):
    for step in range(STEPS):
        mean = lax.optimization_barrier(jnp.sum(composition_vector, axis=0)) / FIELDS

        def one_field(pair):
            current, wiener = pair
            padded = jnp.concatenate([current[:, -1:], current, current[:, :1]], axis=1)
            carried_ensemble = transport(padded, current, mean, filtered_motion, spreading_strength, blend_relax_multiplier, wiener)
            return kinetic_yield_term(carried_ensemble, thermal_level, arrhenius_prefactor, ignition_energy_ratio, left_bilinear_weights, right_bilinear_weights, species_yield_weights)
        composition_vector = lax.map(one_field, (composition_vector, brownian_jumps[step]))
    return composition_vector
```

```python
import functools

import jax
import jax.numpy as jnp
from jax import lax
from jax.experimental import pallas as pl
from jax.experimental.pallas import tpu as pltpu
from jax.sharding import PartitionSpec as P

STEPS = 2
SUB = 5
TILE_ROWS = 8

chem_step = 0.2

MESH = pl.DeviceIdType.MESH


def kernel(
    fields,
    spaces,
    wiener,
    inp,
    motion,
    spread,
    blend,
    thermal,
    left_w,
    right_w,
    yield_w,
    prefactor,
    ignition,
    out,
    current1,
    partner_planes,
    chip_half,
    other_sums,
    halo,
    motion_g,
    spread_g,
    blend_g,
    thermal_g,
    arrhenius,
    left_p,
    right_p,
    yield_p,
    column,
    pre_b,
    ign_b,
    flow_send,
    flow_recv,
    pair_send,
    pair_recv,
    cross_send,
    cross_recv,
    relay_send,
    relay_recv,
    halo_send,
    halo_recv,
):
    planes, rows, species, lanes = inp.shape
    reactions = left_w.shape[0]
    padded = left_p.shape[0]
    half = rows // 2
    chips = fields // 2
    local_rows = spread.shape[1]
    me = lax.axis_index("field")
    slab = lax.axis_index("space")
    core = lax.rem(me, 2)
    chip = lax.div(me, 2)
    partner = chip * 2 + 1 - core
    right = lax.rem(slab + 1, spaces)
    left = lax.rem(slab + spaces - 1, spaces)
    mine = pl.ds(core * half, half)
    others = pl.ds((1 - core) * half, half)
    order = list(range(1, planes - 1)) + [0, planes - 1]

    barrier = pltpu.get_barrier_semaphore()
    for d in range(1, fields):
        pl.semaphore_signal(
            barrier, inc=1, device_id={"field": lax.rem(me + d, fields)}, device_id_type=MESH
        )
    for neighbour in (left, right):
        pl.semaphore_signal(barrier, inc=1, device_id={"space": neighbour}, device_id_type=MESH)
    pl.semaphore_wait(barrier, fields + 1)

    def remote(src, dst, send, recv, **to):
        return pltpu.make_async_remote_copy(
            src_ref=src,
            dst_ref=dst,
            send_sem=send,
            recv_sem=recv,
            device_id=to,
            device_id_type=MESH,
        )

    sources = [inp, current1]

    def pair_copy(step, p):
        return remote(
            sources[step].at[p],
            partner_planes.at[step, p],
            pair_send.at[step, p],
            pair_recv.at[step, p],
            field=partner,
        )

    def cross_copy(step, p, d):
        return remote(
            chip_half.at[step, p],
            other_sums.at[step, p, d - 1, mine],
            cross_send.at[step, p, d - 1],
            cross_recv.at[step, p, d - 1],
            field=lax.rem(chip + d, chips) * 2 + core,
        )

    def relay_copy(step, p, d):
        return remote(
            other_sums.at[step, p, d - 1, mine],
            other_sums.at[step, p, d - 1, mine],
            relay_send.at[step, p, d - 1],
            relay_recv.at[step, p, d - 1],
            field=partner,
        )

    def halo_copy(step, side):
        return remote(
            sources[step].at[planes - 1 if side == 0 else 0],
            halo.at[step, side],
            halo_send.at[step, side],
            halo_recv.at[step, side],
            space=right if side == 0 else left,
        )

    flow_pairs = [(thermal, thermal_g), (motion, motion_g), (spread, spread_g), (blend, blend_g)]

    def flow_copy(k, d):
        src, dst = flow_pairs[k]
        return remote(
            src,
            dst.at[me],
            flow_send.at[k, d - 1],
            flow_recv.at[k, d - 1],
            field=lax.rem(me + d, fields),
        )

    pair_copy(0, order[0]).start()
    for k in range(4):
        for d in range(1, fields):
            flow_copy(k, d).start()
    for p in order[1:]:
        pair_copy(0, p).start()
    for side in range(2):
        halo_copy(0, side).start()
    for src, dst in flow_pairs:
        dst[me] = src[...]

    left_p[...] = jnp.zeros_like(left_p)
    right_p[...] = jnp.zeros_like(right_p)
    yield_p[...] = jnp.zeros_like(yield_p)
    left_p[0:reactions, :] = left_w[...]
    right_p[0:reactions, :] = right_w[...]
    yield_p[:, 0:reactions] = yield_w[...]
    for src, dst in ((prefactor, pre_b), (ignition, ign_b)):
        column[...] = jnp.zeros_like(column)
        column[0:1, 0:reactions] = src[...]
        spread_rows = jnp.broadcast_to(column[0:1, :], (lanes, column.shape[1]))
        dst[...] = jnp.transpose(spread_rows)[0:padded, :]

    def reduce_pair(step, p):
        pair_copy(step, p).wait_recv()
        chip_half[step, p] = sources[step][p, mine] + partner_planes[step, p, mine]

    def send_cross(step, p):
        for d in range(1, chips):
            cross_copy(step, p, d).start()

    def relay(step, p):
        for d in range(1, chips):
            cross_copy(step, p, d).wait_recv()
            relay_copy(step, p, d).start()

    for i, p in enumerate(order):
        reduce_pair(0, p)
        if i > 0:
            send_cross(0, order[i - 1])
    for k in range(4):
        for d in range(1, fields):
            flow_copy(k, d).wait_recv()
    send_cross(0, order[-1])

    def arrhenius_rows(p):
        def one(g, carry):
            for r in range(local_rows):
                inverse = 1.0 / thermal_g[g, p, r : r + 1, :]
                arrhenius[p * rows + g * local_rows + r] = pre_b[...] * jnp.exp(
                    -(ign_b[...] * jnp.broadcast_to(inverse, (padded, lanes)))
                )
            return carry

        lax.fori_loop(0, fields, one, 0)

    def transport(step, p, dst):
        src = sources[step]
        before = halo.at[step, 0] if p == 0 else src.at[p - 1]
        after = halo.at[step, 1] if p == planes - 1 else src.at[p + 1]
        w = [wiener[step, 0, k] for k in range(3)]

        def one(g, carry):
            for r in range(local_rows):
                y = g * local_rows + r
                d_row = spread_g[g, p, r : r + 1, :]
                mix = blend_g[g, p, r : r + 1, :]
                noise = jnp.sqrt(2.0 * d_row)
                e = [0.5 * (motion_g[g, k, p, r : r + 1, :] - noise * w[k]) for k in range(3)]
                centre = 1.0 - 6.0 * d_row - mix
                own = src[p, y]
                y_up = src[p, lax.rem(y + 1, rows)]
                y_down = src[p, lax.rem(y + rows - 1, rows)]
                total = own + partner_planes[step, p, y]
                for d in range(1, chips):
                    total = total + other_sums[step, p, d - 1, y]
                moved = centre * own + (mix * (1.0 / fields)) * total
                moved = moved + (d_row - e[0]) * after[y] + (d_row + e[0]) * before[y]
                moved = moved + (d_row - e[1]) * y_up + (d_row + e[1]) * y_down
                moved = moved + (d_row - e[2]) * pltpu.roll(own, lanes - 1, 1)
                moved = moved + (d_row + e[2]) * pltpu.roll(own, 1, 1)
                dst[p, y] = moved
            return carry

        lax.fori_loop(0, fields, one, 0)

    def chemistry(p, first, last, dst):
        def one(substep, carry):
            for base in range(0, rows, TILE_ROWS):
                block = jnp.concatenate([dst[p, base + i] for i in range(TILE_ROWS)], axis=1)
                low = block.astype(jnp.bfloat16)
                forward = jnp.dot(left_p[...], low, preferred_element_type=jnp.float32)
                backward = jnp.dot(right_p[...], low, preferred_element_type=jnp.float32)
                level = jnp.concatenate(
                    [arrhenius[p * rows + base + i] for i in range(TILE_ROWS)], axis=1
                )
                saturation = 1.0 + forward * forward + backward * backward
                rates = (level * forward * backward / saturation).astype(jnp.bfloat16)
                block = block + chem_step * jnp.dot(
                    yield_p[:, 0:padded], rates, preferred_element_type=jnp.float32
                )
                for i in range(TILE_ROWS):
                    dst[p, base + i] = block[:, i * lanes : (i + 1) * lanes]
            return carry

        lax.fori_loop(first, last, one, 0)

    for p in order[:1]:
        arrhenius_rows(p)
    relay(0, order[0])
    for p in order[1:]:
        arrhenius_rows(p)

    middle = SUB // 2
    for k in range(STEPS * planes):
        step, i = divmod(k, planes)
        p = order[i]
        dst = current1 if step < STEPS - 1 else out
        for d in range(1, chips):
            relay_copy(step, p, d).wait_recv()
        if p == 0:
            halo_copy(step, 0).wait_recv()
        if p == planes - 1:
            halo_copy(step, 1).wait_recv()
        transport(step, p, dst)
        chemistry(p, 0, middle, dst)
        if k < planes - 1:
            relay(0, order[k + 1])
        if 2 <= k < planes + 2:
            relay(1, order[k - 2])
        if 1 <= k < planes + 1:
            reduce_pair(1, order[k - 1])
        chemistry(p, middle, SUB, dst)
        if 1 <= k < planes + 1:
            send_cross(1, order[k - 1])
        if step == 0:
            pair_copy(1, p).start()
            if p == planes - 1:
                halo_copy(1, 0).start()
            if p == 0:
                halo_copy(1, 1).start()

    for step in range(STEPS):
        for p in range(planes):
            pair_copy(step, p).wait_send()
            for d in range(1, chips):
                cross_copy(step, p, d).wait_send()
                relay_copy(step, p, d).wait_send()
        for side in range(2):
            halo_copy(step, side).wait_send()
    for k in range(4):
        for d in range(1, fields):
            flow_copy(k, d).wait_send()


def body(
    fields,
    spaces,
    composition_vector,
    filtered_motion,
    spreading_strength,
    blend_relax_multiplier,
    thermal_level,
    brownian_jumps,
    left_bilinear_weights,
    right_bilinear_weights,
    species_yield_weights,
    arrhenius_prefactor,
    ignition_energy_ratio,
):
    _, species, planes, rows, lanes = composition_vector.shape
    reactions = left_bilinear_weights.shape[0]
    padded = -(-reactions // 16) * 16
    wide = -(-padded // 128) * 128
    local_rows = spreading_strength.shape[1]
    chips = fields // 2
    others = max(chips - 1, 1)
    f32 = jnp.float32
    vmem = pl.BlockSpec(memory_space=pltpu.VMEM)
    state = jnp.transpose(composition_vector[0], (1, 2, 0, 3))
    result = pl.pallas_call(
        functools.partial(kernel, fields, spaces),
        out_shape=jax.ShapeDtypeStruct(state.shape, f32),
        in_specs=[pl.BlockSpec(memory_space=pltpu.SMEM)] + [vmem] * 10,
        out_specs=vmem,
        scratch_shapes=[
            pltpu.VMEM((planes, rows, species, lanes), f32),
            pltpu.VMEM((STEPS, planes, rows, species, lanes), f32),
            pltpu.VMEM((STEPS, planes, rows // 2, species, lanes), f32),
            pltpu.VMEM((STEPS, planes, others, rows, species, lanes), f32),
            pltpu.VMEM((STEPS, 2, rows, species, lanes), f32),
            pltpu.VMEM((fields, 3, planes, local_rows, lanes), f32),
            pltpu.VMEM((fields, planes, local_rows, lanes), f32),
            pltpu.VMEM((fields, planes, local_rows, lanes), f32),
            pltpu.VMEM((fields, planes, local_rows, lanes), f32),
            pltpu.VMEM((planes * rows, padded, lanes), f32),
            pltpu.VMEM((padded, species), jnp.bfloat16),
            pltpu.VMEM((padded, species), jnp.bfloat16),
            pltpu.VMEM((species, wide), jnp.bfloat16),
            pltpu.VMEM((8, wide), f32),
            pltpu.VMEM((padded, lanes), f32),
            pltpu.VMEM((padded, lanes), f32),
            pltpu.SemaphoreType.DMA((4, fields)),
            pltpu.SemaphoreType.DMA((4, fields)),
            pltpu.SemaphoreType.DMA((STEPS, planes)),
            pltpu.SemaphoreType.DMA((STEPS, planes)),
            pltpu.SemaphoreType.DMA((STEPS, planes, others)),
            pltpu.SemaphoreType.DMA((STEPS, planes, others)),
            pltpu.SemaphoreType.DMA((STEPS, planes, others)),
            pltpu.SemaphoreType.DMA((STEPS, planes, others)),
            pltpu.SemaphoreType.DMA((STEPS, 2)),
            pltpu.SemaphoreType.DMA((STEPS, 2)),
        ],
        compiler_params=pltpu.CompilerParams(
            collective_id=0, has_side_effects=True, vmem_limit_bytes=60 * 1024 * 1024
        ),
        name="fields_step",
    )(
        brownian_jumps,
        state,
        filtered_motion,
        spreading_strength,
        blend_relax_multiplier,
        thermal_level,
        left_bilinear_weights,
        right_bilinear_weights,
        species_yield_weights,
        arrhenius_prefactor[None],
        ignition_energy_ratio[None],
    )
    return jnp.transpose(result, (2, 0, 1, 3))[None]


def solution(mesh):
    return jax.shard_map(
        functools.partial(body, mesh.shape["field"], mesh.shape["space"]),
        mesh=mesh,
        in_specs=(
            P("field", None, "space", None, None),
            P(None, "space", "field", None),
            P("space", "field", None),
            P("space", "field", None),
            P("space", "field", None),
            P(None, "field", None),
            P(),
            P(),
            P(),
            P(),
            P(),
        ),
        out_specs=P("field", None, "space", None, None),
        check_vma=False,
    )
```

```python
import functools

import jax
import jax.numpy as jnp
from jax import lax
from jax.experimental import pallas as pl
from jax.experimental.pallas import tpu as pltpu
from jax.sharding import PartitionSpec as P

STEPS = 2
SUB = 5
TILE_ROWS = 8

chem_step = 0.2

MESH = pl.DeviceIdType.MESH


def kernel(
    fields,
    spaces,
    wiener,
    given,
    motion,
    spread,
    blend,
    thermal,
    left_w,
    right_w,
    yield_w,
    prefactor,
    ignition,
    out,
    current0,
    current1,
    current2,
    partner_planes,
    chip_half,
    other_sums,
    halo,
    motion_g,
    spread_g,
    blend_g,
    thermal_g,
    arrhenius,
    both_p,
    yield_p,
    column,
    pre_b,
    ign_b,
    flow_send,
    flow_recv,
    pair_send,
    pair_recv,
    cross_send,
    cross_recv,
    relay_send,
    relay_recv,
    halo_send,
    halo_recv,
):
    planes, rows, species, lanes = current0.shape
    reactions = left_w.shape[1]
    padded = pre_b.shape[0]
    stride = planes * rows
    half = rows // 2
    chips = fields // 2
    local_rows = spread.shape[1]
    me = lax.axis_index("field")
    slab = lax.axis_index("space")
    core = lax.rem(me, 2)
    chip = lax.div(me, 2)
    partner = chip * 2 + 1 - core
    right = lax.rem(slab + 1, spaces)
    left = lax.rem(slab + spaces - 1, spaces)
    mine = pl.ds(core * half, half)
    others = pl.ds((1 - core) * half, half)
    order = list(range(1, planes - 1)) + [0, planes - 1]

    barrier = pltpu.get_barrier_semaphore()
    for d in range(1, fields):
        pl.semaphore_signal(
            barrier, inc=1, device_id={"field": lax.rem(me + d, fields)}, device_id_type=MESH
        )
    for neighbour in (left, right):
        pl.semaphore_signal(barrier, inc=1, device_id={"space": neighbour}, device_id_type=MESH)

    def relayout(t, carry):
        current0[t // rows, lax.rem(t, rows)] = given[pl.ds(t, species, stride=stride), :]
        return carry

    lax.fori_loop(0, stride, relayout, 0, unroll=4)
    pl.semaphore_wait(barrier, fields + 1)

    def remote(src, dst, send, recv, **to):
        return pltpu.make_async_remote_copy(
            src_ref=src,
            dst_ref=dst,
            send_sem=send,
            recv_sem=recv,
            device_id=to,
            device_id_type=MESH,
        )

    sources = [current0, current1]

    def pair_copy(step, p):
        return remote(
            sources[step].at[p],
            partner_planes.at[step, p],
            pair_send.at[step, p],
            pair_recv.at[step, p],
            field=partner,
        )

    def cross_copy(step, p, d):
        return remote(
            chip_half.at[step, p],
            other_sums.at[step, p, d - 1, mine],
            cross_send.at[step, p, d - 1],
            cross_recv.at[step, p, d - 1],
            field=lax.rem(chip + d, chips) * 2 + core,
        )

    def relay_copy(step, p, d):
        return remote(
            other_sums.at[step, p, d - 1, mine],
            other_sums.at[step, p, d - 1, mine],
            relay_send.at[step, p, d - 1],
            relay_recv.at[step, p, d - 1],
            field=partner,
        )

    def halo_copy(step, side):
        return remote(
            sources[step].at[planes - 1 if side == 0 else 0],
            halo.at[step, side],
            halo_send.at[step, side],
            halo_recv.at[step, side],
            space=right if side == 0 else left,
        )

    flow_pairs = [(thermal, thermal_g), (motion, motion_g), (spread, spread_g), (blend, blend_g)]

    def flow_copy(k, d):
        src, dst = flow_pairs[k]
        return remote(
            src,
            dst.at[me],
            flow_send.at[k, d - 1],
            flow_recv.at[k, d - 1],
            field=lax.rem(me + d, fields),
        )

    def reduce_pair(step, p):
        pair_copy(step, p).wait_recv()
        chip_half[step, p] = sources[step][p, mine] + partner_planes[step, p, mine]

    def send_cross(step, p):
        for d in range(1, chips):
            cross_copy(step, p, d).start()

    def relay(step, p):
        for d in range(1, chips):
            cross_copy(step, p, d).wait_recv()
            relay_copy(step, p, d).start()

    pair_copy(0, order[0]).start()
    for d in range(1, fields):
        flow_copy(0, d).start()
    for p in order[1:]:
        pair_copy(0, p).start()
    for k in range(1, 4):
        for d in range(1, fields):
            flow_copy(k, d).start()
    for side in range(2):
        halo_copy(0, side).start()
    for src, dst in flow_pairs:
        dst[me] = src[...]

    reduce_pair(0, order[0])
    column[...] = jnp.zeros_like(column)
    for k, src in enumerate((left_w, right_w)):
        column[0:species, 0:reactions] = src[...].astype(jnp.float32)
        turned = jnp.transpose(column[...])
        both_p[k * padded : (k + 1) * padded, :] = turned[0:padded, 0:species].astype(jnp.bfloat16)
    yield_p[...] = jnp.zeros_like(yield_p)
    yield_p[:, 0:reactions] = yield_w[...]
    send_cross(0, order[0])
    for src, dst in ((prefactor, pre_b), (ignition, ign_b)):
        column[0:1, 0:reactions] = src[...]
        dst[...] = jnp.transpose(jnp.broadcast_to(column[0:1, :], column.shape))[0:padded, :]
    for i, p in enumerate(order[1:]):
        reduce_pair(0, p)
        if i > 0:
            send_cross(0, order[i])
    for k in range(4):
        for d in range(1, fields):
            flow_copy(k, d).wait_recv()
    send_cross(0, order[-1])

    def arrhenius_rows(p):
        def one(g, carry):
            for r in range(local_rows):
                inverse = 1.0 / thermal_g[g, p, r : r + 1, :]
                arrhenius[p * rows + g * local_rows + r] = pre_b[...] * jnp.exp(
                    -(ign_b[...] * jnp.broadcast_to(inverse, (padded, lanes)))
                )
            return carry

        lax.fori_loop(0, fields, one, 0)

    def transport(step, p, dst):
        src = sources[step]
        before = halo.at[step, 0] if p == 0 else src.at[p - 1]
        after = halo.at[step, 1] if p == planes - 1 else src.at[p + 1]
        w = [wiener[step, 0, k] for k in range(3)]

        def one(g, carry):
            for r in range(local_rows):
                y = g * local_rows + r
                d_row = spread_g[g, p, r : r + 1, :]
                mix = blend_g[g, p, r : r + 1, :]
                noise = jnp.sqrt(2.0 * d_row)
                e = [0.5 * (motion_g[g, k, p, r : r + 1, :] - noise * w[k]) for k in range(3)]
                centre = 1.0 - 6.0 * d_row - mix
                own = src[p, y]
                y_up = src[p, lax.rem(y + 1, rows)]
                y_down = src[p, lax.rem(y + rows - 1, rows)]
                total = own + partner_planes[step, p, y]
                for d in range(1, chips):
                    total = total + other_sums[step, p, d - 1, y]
                moved = centre * own + (mix * (1.0 / fields)) * total
                moved = moved + (d_row - e[0]) * after[y] + (d_row + e[0]) * before[y]
                moved = moved + (d_row - e[1]) * y_up + (d_row + e[1]) * y_down
                moved = moved + (d_row - e[2]) * pltpu.roll(own, lanes - 1, 1)
                moved = moved + (d_row + e[2]) * pltpu.roll(own, 1, 1)
                dst[p, y] = moved
            return carry

        lax.fori_loop(0, fields, one, 0)

    def chemistry(p, first, last, dst):
        def one(substep, carry):
            def settle(base, block, rates):
                block = block + chem_step * jnp.dot(
                    yield_p[:, 0:padded], rates, preferred_element_type=jnp.float32
                )
                for i in range(TILE_ROWS):
                    dst[p, base + i] = block[:, i * lanes : (i + 1) * lanes]

            pending = None
            for base in range(0, rows, TILE_ROWS):
                block = jnp.concatenate([dst[p, base + i] for i in range(TILE_ROWS)], axis=1)
                factors = jnp.dot(
                    both_p[...], block.astype(jnp.bfloat16), preferred_element_type=jnp.float32
                )
                forward, backward = factors[:padded], factors[padded:]
                level = jnp.concatenate(
                    [arrhenius[p * rows + base + i] for i in range(TILE_ROWS)], axis=1
                )
                saturation = 1.0 + forward * forward + backward * backward
                rates = (level * forward * backward / saturation).astype(jnp.bfloat16)
                if pending is not None:
                    settle(*pending)
                pending = (base, block, rates)
            settle(*pending)
            return carry

        lax.fori_loop(first, last, one, 0)

    for p in order[:1]:
        arrhenius_rows(p)
    relay(0, order[0])
    for p in order[1:]:
        arrhenius_rows(p)

    middle = SUB // 2
    for k in range(STEPS * planes):
        step, i = divmod(k, planes)
        p = order[i]
        dst = current1 if step < STEPS - 1 else current2
        for d in range(1, chips):
            relay_copy(step, p, d).wait_recv()
        if p == 0:
            halo_copy(step, 0).wait_recv()
        if p == planes - 1:
            halo_copy(step, 1).wait_recv()
        transport(step, p, dst)
        chemistry(p, 0, middle, dst)
        if k < planes - 1:
            relay(0, order[k + 1])
        if 2 <= k < planes + 2:
            relay(1, order[k - 2])
        if 1 <= k < planes + 1:
            reduce_pair(1, order[k - 1])
        chemistry(p, middle, SUB, dst)
        if 1 <= k < planes + 1:
            send_cross(1, order[k - 1])
        if step == STEPS - 1:

            def finish(y, carry):
                out[pl.ds(p * rows + y, species, stride=stride), :] = current2[p, y]
                return carry

            lax.fori_loop(0, rows, finish, 0, unroll=4)
        if step == 0:
            pair_copy(1, p).start()
            if p == planes - 1:
                halo_copy(1, 0).start()
            if p == 0:
                halo_copy(1, 1).start()

    for step in range(STEPS):
        for p in range(planes):
            pair_copy(step, p).wait_send()
            for d in range(1, chips):
                cross_copy(step, p, d).wait_send()
                relay_copy(step, p, d).wait_send()
        for side in range(2):
            halo_copy(step, side).wait_send()
    for k in range(4):
        for d in range(1, fields):
            flow_copy(k, d).wait_send()


def body(
    fields,
    spaces,
    composition_vector,
    filtered_motion,
    spreading_strength,
    blend_relax_multiplier,
    thermal_level,
    brownian_jumps,
    left_bilinear_weights,
    right_bilinear_weights,
    species_yield_weights,
    arrhenius_prefactor,
    ignition_energy_ratio,
):
    _, species, planes, rows, lanes = composition_vector.shape
    reactions = left_bilinear_weights.shape[0]
    padded = -(-reactions // 16) * 16
    wide = -(-padded // 128) * 128
    local_rows = spreading_strength.shape[1]
    chips = fields // 2
    others = max(chips - 1, 1)
    f32 = jnp.float32
    vmem = pl.BlockSpec(memory_space=pltpu.VMEM)
    state = composition_vector.reshape(species * planes * rows, lanes)
    result = pl.pallas_call(
        functools.partial(kernel, fields, spaces),
        out_shape=jax.ShapeDtypeStruct(state.shape, f32),
        in_specs=[pl.BlockSpec(memory_space=pltpu.SMEM)] + [vmem] * 10,
        out_specs=vmem,
        scratch_shapes=[
            pltpu.VMEM((planes, rows, species, lanes), f32),
            pltpu.VMEM((planes, rows, species, lanes), f32),
            pltpu.VMEM((planes, rows, species, lanes), f32),
            pltpu.VMEM((STEPS, planes, rows, species, lanes), f32),
            pltpu.VMEM((STEPS, planes, rows // 2, species, lanes), f32),
            pltpu.VMEM((STEPS, planes, others, rows, species, lanes), f32),
            pltpu.VMEM((STEPS, 2, rows, species, lanes), f32),
            pltpu.VMEM((fields, 3, planes, local_rows, lanes), f32),
            pltpu.VMEM((fields, planes, local_rows, lanes), f32),
            pltpu.VMEM((fields, planes, local_rows, lanes), f32),
            pltpu.VMEM((fields, planes, local_rows, lanes), f32),
            pltpu.VMEM((planes * rows, padded, lanes), f32),
            pltpu.VMEM((2 * padded, species), jnp.bfloat16),
            pltpu.VMEM((species, wide), jnp.bfloat16),
            pltpu.VMEM((lanes, wide), f32),
            pltpu.VMEM((padded, lanes), f32),
            pltpu.VMEM((padded, lanes), f32),
            pltpu.SemaphoreType.DMA((4, fields)),
            pltpu.SemaphoreType.DMA((4, fields)),
            pltpu.SemaphoreType.DMA((STEPS, planes)),
            pltpu.SemaphoreType.DMA((STEPS, planes)),
            pltpu.SemaphoreType.DMA((STEPS, planes, others)),
            pltpu.SemaphoreType.DMA((STEPS, planes, others)),
            pltpu.SemaphoreType.DMA((STEPS, planes, others)),
            pltpu.SemaphoreType.DMA((STEPS, planes, others)),
            pltpu.SemaphoreType.DMA((STEPS, 2)),
            pltpu.SemaphoreType.DMA((STEPS, 2)),
        ],
        compiler_params=pltpu.CompilerParams(
            collective_id=0, has_side_effects=True, vmem_limit_bytes=60 * 1024 * 1024
        ),
        name="fields_step",
    )(
        brownian_jumps,
        state,
        filtered_motion,
        spreading_strength,
        blend_relax_multiplier,
        thermal_level,
        left_bilinear_weights.T,
        right_bilinear_weights.T,
        species_yield_weights,
        arrhenius_prefactor[None],
        ignition_energy_ratio[None],
    )
    return result.reshape(composition_vector.shape)


def solution(mesh):
    return jax.shard_map(
        functools.partial(body, mesh.shape["field"], mesh.shape["space"]),
        mesh=mesh,
        in_specs=(
            P("field", None, "space", None, None),
            P(None, "space", "field", None),
            P("space", "field", None),
            P("space", "field", None),
            P("space", "field", None),
            P(None, "field", None),
            P(),
            P(),
            P(),
            P(),
            P(),
        ),
        out_specs=P("field", None, "space", None, None),
        check_vma=False,
    )
```

```python
import functools

import jax
import jax.numpy as jnp
from jax import lax
from jax.experimental import pallas as pl
from jax.experimental.pallas import tpu as pltpu
from jax.sharding import PartitionSpec as P

STEPS = 2
SUB = 5
TILE_ROWS = 8

chem_step = 0.2

MESH = pl.DeviceIdType.MESH


def kernel(
    fields,
    spaces,
    wiener,
    given,
    motion,
    spread,
    blend,
    thermal,
    left_w,
    right_w,
    yield_w,
    prefactor,
    ignition,
    out,
    current0,
    current1,
    current2,
    partner_planes,
    chip_half,
    other_sums,
    halo,
    motion_g,
    spread_g,
    blend_g,
    thermal_g,
    arrhenius,
    both_p,
    yield_p,
    column,
    pre_b,
    ign_b,
    flow_send,
    flow_recv,
    pair_send,
    pair_recv,
    cross_send,
    cross_recv,
    relay_send,
    relay_recv,
    halo_send,
    halo_recv,
):
    planes, rows, species, lanes = current0.shape
    reactions = left_w.shape[1]
    padded = pre_b.shape[0]
    stride = planes * rows
    half = rows // 2
    chips = fields // 2
    local_rows = spread.shape[1]
    me = lax.axis_index("field")
    slab = lax.axis_index("space")
    core = lax.rem(me, 2)
    chip = lax.div(me, 2)
    partner = chip * 2 + 1 - core
    right = lax.rem(slab + 1, spaces)
    left = lax.rem(slab + spaces - 1, spaces)
    mine = pl.ds(core * half, half)
    others = pl.ds((1 - core) * half, half)
    order = list(range(1, planes - 1)) + [0, planes - 1]

    barrier = pltpu.get_barrier_semaphore()
    for d in range(1, fields):
        pl.semaphore_signal(
            barrier, inc=1, device_id={"field": lax.rem(me + d, fields)}, device_id_type=MESH
        )
    for neighbour in (left, right):
        pl.semaphore_signal(barrier, inc=1, device_id={"space": neighbour}, device_id_type=MESH)

    def relayout(t, carry):
        current0[t // rows, lax.rem(t, rows)] = given[pl.ds(t, species, stride=stride), :]
        return carry

    lax.fori_loop(0, stride, relayout, 0, unroll=4)
    pl.semaphore_wait(barrier, fields + 1)

    def remote(src, dst, send, recv, **to):
        return pltpu.make_async_remote_copy(
            src_ref=src,
            dst_ref=dst,
            send_sem=send,
            recv_sem=recv,
            device_id=to,
            device_id_type=MESH,
        )

    sources = [current0, current1]

    def pair_copy(step, p):
        return remote(
            sources[step].at[p],
            partner_planes.at[step, p],
            pair_send.at[step, p],
            pair_recv.at[step, p],
            field=partner,
        )

    def cross_copy(step, p, d):
        return remote(
            chip_half.at[step, p],
            other_sums.at[step, p, d - 1, mine],
            cross_send.at[step, p, d - 1],
            cross_recv.at[step, p, d - 1],
            field=lax.rem(chip + d, chips) * 2 + core,
        )

    def relay_copy(step, p, d):
        return remote(
            other_sums.at[step, p, d - 1, mine],
            other_sums.at[step, p, d - 1, mine],
            relay_send.at[step, p, d - 1],
            relay_recv.at[step, p, d - 1],
            field=partner,
        )

    def halo_copy(step, side):
        return remote(
            sources[step].at[planes - 1 if side == 0 else 0],
            halo.at[step, side],
            halo_send.at[step, side],
            halo_recv.at[step, side],
            space=right if side == 0 else left,
        )

    flow_pairs = [(thermal, thermal_g), (motion, motion_g), (spread, spread_g), (blend, blend_g)]

    def flow_copy(k, d):
        src, dst = flow_pairs[k]
        return remote(
            src,
            dst.at[me],
            flow_send.at[k, d - 1],
            flow_recv.at[k, d - 1],
            field=lax.rem(me + d, fields),
        )

    def reduce_pair(step, p):
        pair_copy(step, p).wait_recv()
        chip_half[step, p] = sources[step][p, mine] + partner_planes[step, p, mine]

    def send_cross(step, p):
        for d in range(1, chips):
            cross_copy(step, p, d).start()

    def relay(step, p):
        for d in range(1, chips):
            cross_copy(step, p, d).wait_recv()
            relay_copy(step, p, d).start()

    pair_copy(0, order[0]).start()
    for d in range(1, fields):
        flow_copy(0, d).start()
    for p in order[1:]:
        pair_copy(0, p).start()
    for side in range(2):
        halo_copy(0, side).start()
    for src, dst in flow_pairs:
        dst[me] = src[...]

    reduce_pair(0, order[0])
    column[...] = jnp.zeros_like(column)
    for k, src in enumerate((left_w, right_w)):
        column[0:species, 0:reactions] = src[...].astype(jnp.float32)
        turned = jnp.transpose(column[...])
        both_p[k * padded : (k + 1) * padded, :] = turned[0:padded, 0:species].astype(jnp.bfloat16)
    yield_p[...] = jnp.zeros_like(yield_p)
    yield_p[:, 0:reactions] = yield_w[...]
    send_cross(0, order[0])
    for k in range(1, 4):
        for d in range(1, fields):
            flow_copy(k, d).start()
    for src, dst in ((prefactor, pre_b), (ignition, ign_b)):
        column[0:1, 0:reactions] = src[...]
        dst[...] = jnp.transpose(jnp.broadcast_to(column[0:1, :], column.shape))[0:padded, :]
    for i, p in enumerate(order[1:]):
        reduce_pair(0, p)
        if i > 0:
            send_cross(0, order[i])
    for d in range(1, fields):
        flow_copy(0, d).wait_recv()
    send_cross(0, order[-1])

    def arrhenius_rows(p):
        def one(g, carry):
            for r in range(local_rows):
                inverse = 1.0 / thermal_g[g, p, r : r + 1, :]
                arrhenius[p * rows + g * local_rows + r] = pre_b[...] * jnp.exp(
                    -(ign_b[...] * jnp.broadcast_to(inverse, (padded, lanes)))
                )
            return carry

        lax.fori_loop(0, fields, one, 0)

    def transport(step, p, dst):
        src = sources[step]
        before = halo.at[step, 0] if p == 0 else src.at[p - 1]
        after = halo.at[step, 1] if p == planes - 1 else src.at[p + 1]
        w = [wiener[step, 0, k] for k in range(3)]

        def one(g, carry):
            for r in range(local_rows):
                y = g * local_rows + r
                d_row = spread_g[g, p, r : r + 1, :]
                mix = blend_g[g, p, r : r + 1, :]
                noise = jnp.sqrt(2.0 * d_row)
                e = [0.5 * (motion_g[g, k, p, r : r + 1, :] - noise * w[k]) for k in range(3)]
                centre = 1.0 - 6.0 * d_row - mix
                own = src[p, y]
                y_up = src[p, lax.rem(y + 1, rows)]
                y_down = src[p, lax.rem(y + rows - 1, rows)]
                total = own + partner_planes[step, p, y]
                for d in range(1, chips):
                    total = total + other_sums[step, p, d - 1, y]
                moved = centre * own + (mix * (1.0 / fields)) * total
                moved = moved + (d_row - e[0]) * after[y] + (d_row + e[0]) * before[y]
                moved = moved + (d_row - e[1]) * y_up + (d_row + e[1]) * y_down
                moved = moved + (d_row - e[2]) * pltpu.roll(own, lanes - 1, 1)
                moved = moved + (d_row + e[2]) * pltpu.roll(own, 1, 1)
                dst[p, y] = moved
            return carry

        lax.fori_loop(0, fields, one, 0)

    def chemistry(p, first, last, dst):
        def one(substep, carry):
            def settle(base, block, rates):
                block = block + chem_step * jnp.dot(
                    yield_p[:, 0:padded], rates, preferred_element_type=jnp.float32
                )
                for i in range(TILE_ROWS):
                    dst[p, base + i] = block[:, i * lanes : (i + 1) * lanes]

            pending = None
            for base in range(0, rows, TILE_ROWS):
                block = jnp.concatenate([dst[p, base + i] for i in range(TILE_ROWS)], axis=1)
                factors = jnp.dot(
                    both_p[...], block.astype(jnp.bfloat16), preferred_element_type=jnp.float32
                )
                forward, backward = factors[:padded], factors[padded:]
                level = jnp.concatenate(
                    [arrhenius[p * rows + base + i] for i in range(TILE_ROWS)], axis=1
                )
                saturation = 1.0 + forward * forward + backward * backward
                rates = (level * forward * backward / saturation).astype(jnp.bfloat16)
                if pending is not None:
                    settle(*pending)
                pending = (base, block, rates)
            settle(*pending)
            return carry

        lax.fori_loop(first, last, one, 0)

    for p in order[:1]:
        arrhenius_rows(p)
    relay(0, order[0])
    for p in order[1:]:
        arrhenius_rows(p)
    for k in range(1, 4):
        for d in range(1, fields):
            flow_copy(k, d).wait_recv()

    middle = SUB // 2
    late_order = list(range(1, planes - 1)) + [planes - 1, 0]
    for k in range(STEPS * planes):
        step, i = divmod(k, planes)
        p = order[i] if step == 0 else late_order[i]
        dst = current1 if step < STEPS - 1 else current2
        for d in range(1, chips):
            relay_copy(step, p, d).wait_recv()
        if p == 0:
            halo_copy(step, 0).wait_recv()
        if p == planes - 1:
            halo_copy(step, 1).wait_recv()
        transport(step, p, dst)
        chemistry(p, 0, middle, dst)
        if 1 <= k < planes + 1:
            reduce_pair(1, order[k - 1])
        if k < planes - 1:
            relay(0, order[k + 1])
        if 3 <= k < planes + 2:
            relay(1, order[k - 3])
        if 1 <= k < planes + 1:
            send_cross(1, order[k - 1])
        if k == planes + 1:
            relay(1, order[planes - 1])
        chemistry(p, middle, SUB, dst)
        if step == STEPS - 1:

            def finish(y, carry):
                out[pl.ds(p * rows + y, species, stride=stride), :] = current2[p, y]
                return carry

            lax.fori_loop(0, rows, finish, 0, unroll=4)
        if step == 0:
            pair_copy(1, p).start()
            if p == planes - 1:
                halo_copy(1, 0).start()
            if p == 0:
                halo_copy(1, 1).start()

    for step in range(STEPS):
        for p in range(planes):
            pair_copy(step, p).wait_send()
            for d in range(1, chips):
                cross_copy(step, p, d).wait_send()
                relay_copy(step, p, d).wait_send()
        for side in range(2):
            halo_copy(step, side).wait_send()
    for k in range(4):
        for d in range(1, fields):
            flow_copy(k, d).wait_send()


def body(
    fields,
    spaces,
    composition_vector,
    filtered_motion,
    spreading_strength,
    blend_relax_multiplier,
    thermal_level,
    brownian_jumps,
    left_bilinear_weights,
    right_bilinear_weights,
    species_yield_weights,
    arrhenius_prefactor,
    ignition_energy_ratio,
):
    _, species, planes, rows, lanes = composition_vector.shape
    reactions = left_bilinear_weights.shape[0]
    padded = -(-reactions // 16) * 16
    wide = -(-padded // 128) * 128
    local_rows = spreading_strength.shape[1]
    chips = fields // 2
    others = max(chips - 1, 1)
    f32 = jnp.float32
    vmem = pl.BlockSpec(memory_space=pltpu.VMEM)
    state = composition_vector.reshape(species * planes * rows, lanes)
    result = pl.pallas_call(
        functools.partial(kernel, fields, spaces),
        out_shape=jax.ShapeDtypeStruct(state.shape, f32),
        in_specs=[pl.BlockSpec(memory_space=pltpu.SMEM)] + [vmem] * 10,
        out_specs=vmem,
        scratch_shapes=[
            pltpu.VMEM((planes, rows, species, lanes), f32),
            pltpu.VMEM((planes, rows, species, lanes), f32),
            pltpu.VMEM((planes, rows, species, lanes), f32),
            pltpu.VMEM((STEPS, planes, rows, species, lanes), f32),
            pltpu.VMEM((STEPS, planes, rows // 2, species, lanes), f32),
            pltpu.VMEM((STEPS, planes, others, rows, species, lanes), f32),
            pltpu.VMEM((STEPS, 2, rows, species, lanes), f32),
            pltpu.VMEM((fields, 3, planes, local_rows, lanes), f32),
            pltpu.VMEM((fields, planes, local_rows, lanes), f32),
            pltpu.VMEM((fields, planes, local_rows, lanes), f32),
            pltpu.VMEM((fields, planes, local_rows, lanes), f32),
            pltpu.VMEM((planes * rows, padded, lanes), f32),
            pltpu.VMEM((2 * padded, species), jnp.bfloat16),
            pltpu.VMEM((species, wide), jnp.bfloat16),
            pltpu.VMEM((lanes, wide), f32),
            pltpu.VMEM((padded, lanes), f32),
            pltpu.VMEM((padded, lanes), f32),
            pltpu.SemaphoreType.DMA((4, fields)),
            pltpu.SemaphoreType.DMA((4, fields)),
            pltpu.SemaphoreType.DMA((STEPS, planes)),
            pltpu.SemaphoreType.DMA((STEPS, planes)),
            pltpu.SemaphoreType.DMA((STEPS, planes, others)),
            pltpu.SemaphoreType.DMA((STEPS, planes, others)),
            pltpu.SemaphoreType.DMA((STEPS, planes, others)),
            pltpu.SemaphoreType.DMA((STEPS, planes, others)),
            pltpu.SemaphoreType.DMA((STEPS, 2)),
            pltpu.SemaphoreType.DMA((STEPS, 2)),
        ],
        compiler_params=pltpu.CompilerParams(
            collective_id=0, has_side_effects=True, vmem_limit_bytes=60 * 1024 * 1024
        ),
        name="fields_step",
    )(
        brownian_jumps,
        state,
        filtered_motion,
        spreading_strength,
        blend_relax_multiplier,
        thermal_level,
        left_bilinear_weights.T,
        right_bilinear_weights.T,
        species_yield_weights,
        arrhenius_prefactor[None],
        ignition_energy_ratio[None],
    )
    return result.reshape(composition_vector.shape)


def solution(mesh):
    return jax.shard_map(
        functools.partial(body, mesh.shape["field"], mesh.shape["space"]),
        mesh=mesh,
        in_specs=(
            P("field", None, "space", None, None),
            P(None, "space", "field", None),
            P("space", "field", None),
            P("space", "field", None),
            P("space", "field", None),
            P(None, "field", None),
            P(),
            P(),
            P(),
            P(),
            P(),
        ),
        out_specs=P("field", None, "space", None, None),
        check_vma=False,
    )
```
